32 devices in a mesh: tm: 8 (over y, x, core), stream: 4 (over z).
Axes of the slice: x: 2, y: 2, z: 4, core: 2. Of those that a mesh axis runs over, the one named last changes fastest.
Arguments:
- tokens: bfloat16 [4096, 2048], P(('tm', 'stream')), may hold values from -6 to 6
- w_query: bfloat16 [2048, 2048], P('stream'), may hold values from -0.125 to 0.125
- w_key: bfloat16 [2048, 2048], P('stream'), may hold values from -0.125 to 0.125
- w_value: bfloat16 [2048, 2048], P('stream'), may hold values from -0.125 to 0.125
- decay_proj: bfloat16 [2048, 16], P('stream'), may hold values from -0.125 to 0.125
- beta_proj: bfloat16 [2048, 16], P('stream'), may hold values from -0.125 to 0.125
- decay_rate: float32 [16], replicated, may hold values from 0.00024414062 to 0.1
- beta_bias: float32 [16], replicated, may hold values from -7 to 0
- norm_gain: float32 [128], replicated, may hold values from 0.5 to 1.5
Outputs:
- mixed: bfloat16 [4096, 2048], P(('tm', 'stream'))
The draws below stay inside these ranges and needn't reach their ends.
All inputs are finite; a program needn't handle non-finite values.
Results may differ from the reference program's by a relative error of at most 0.0073.
Values may be sent and summed in bfloat16 or wider, within the bound.
A program may use at most 128 MiB of HBM per device.

```python
import math
import jax
import jax.numpy as jnp
from jax import lax

D = 2048
HEADS = 16
DK = 128
DV = 128
GROUP = 256
TOKENS = 4096


def steps_of(rng, dims, split, smallest, largest):
    def one(axis_at, parts):
        heights = jax.random.uniform(jax.random.fold_in(jax.random.fold_in(rng, 6), axis_at), (parts,), jnp.float32, smallest / len(split), largest / len(split))
        return jnp.repeat(jnp.exp(heights), dims[axis_at] // parts).reshape((-1,) + (1,) * (len(dims) - axis_at - 1))

    loudness = one(*split[0])
    for cut in split[1:]:
        loudness = loudness * one(*cut)
    return loudness


def centred(own_key, dims, deviation, limit, cuts=(), held_as=jnp.bfloat16):
    entries = jax.random.normal(own_key, dims, jnp.float32) * deviation
    if len(cuts) > 0:
        entries = steps_of(own_key, dims, cuts, -0.22, 0.18) * entries
    return jnp.clip(entries, min=-limit, max=limit).astype(held_as)


def setup_inputs(seed: int = 0) -> dict:
    key_list = jax.random.split(jax.random.key(seed), 10)
    tokens = centred(key_list[0], (TOKENS, D), 1.0, 6.0, ((0, 32),))
    w_query = centred(key_list[1], (D, HEADS * DK), D ** -0.5, 0.125, ((0, 4),))
    w_key = centred(key_list[2], (D, HEADS * DK), D ** -0.5, 0.125, ((0, 4),))
    w_value = centred(key_list[3], (D, HEADS * DV), D ** -0.5, 0.125, ((0, 4),))
    decay_proj = centred(key_list[4], (D, HEADS), D ** -0.5, 0.125, ((0, 4),))
    beta_proj = centred(key_list[5], (D, HEADS), D ** -0.5, 0.125, ((0, 4),))
    decay_rate = jnp.clip(jnp.exp(jax.random.uniform(key_list[6], (HEADS,), jnp.float32, math.log(0.00024414062), math.log(0.1))), 0.00024414062, 0.1)
    beta_bias = jnp.clip(jax.random.uniform(key_list[7], (HEADS,), jnp.float32, -7.0, 0.0), -7.0, 0.0)
    norm_gain = jnp.clip(1.0 + 0.1 * jax.random.normal(key_list[8], (DV,), jnp.float32), 0.5, 1.5)
    return {"tokens": tokens, "w_query": w_query, "w_key": w_key, "w_value": w_value, "decay_proj": decay_proj, "beta_proj": beta_proj, "decay_rate": decay_rate, "beta_bias": beta_bias, "norm_gain": norm_gain}


highest_precision = lax.Precision.HIGHEST

def narrowed(value):
    return lax.optimization_barrier(value.astype(jnp.bfloat16)).astype(jnp.float32)

def reference(tokens, w_query, w_key, w_value, decay_proj, beta_proj, decay_rate, beta_bias, norm_gain):
    num_blocks = TOKENS // GROUP
    query_mat = w_query.astype(jnp.float32)
    key_mat = w_key.astype(jnp.float32)
    value_mat = w_value.astype(jnp.float32)
    decay_mat_w = decay_proj.astype(jnp.float32)
    beta_mat_w = beta_proj.astype(jnp.float32)
    blocks = tokens.reshape(num_blocks, GROUP, D)
    positions = jnp.arange(GROUP)
    strict = positions[:, None] > positions[None, :]
    inclusive_mask = positions[:, None] >= positions[None, :]
    identity = jnp.eye(GROUP, dtype=jnp.float32)

    def advance(state, block_rows):
        inputs = block_rows.astype(jnp.float32)
        raw_query = jnp.dot(inputs, query_mat, precision=highest_precision).reshape(GROUP, HEADS, DK)
        raw_key = jnp.dot(inputs, key_mat, precision=highest_precision).reshape(GROUP, HEADS, DK)
        queries = narrowed(raw_query * lax.rsqrt(lax.optimization_barrier(jnp.sum(raw_query * raw_query, -1, keepdims=True)) + 1e-06) * DK ** (-0.5))
        key_rows = narrowed(raw_key * lax.rsqrt(lax.optimization_barrier(jnp.sum(raw_key * raw_key, -1, keepdims=True)) + 1e-06))
        values = narrowed(jnp.dot(inputs, value_mat, precision=highest_precision)).reshape(GROUP, HEADS, DV)
        log_decay = narrowed(-decay_rate * jax.nn.softplus(jnp.dot(inputs, decay_mat_w, precision=highest_precision)))
        strength = narrowed(jax.nn.sigmoid(jnp.dot(inputs, beta_mat_w, precision=highest_precision) + beta_bias))
        cumulative = jnp.cumsum(log_decay, axis=0).T
        growth = jnp.exp(cumulative)
        last_log = cumulative[:, -1:]
        tail = jnp.exp(last_log - cumulative)
        strength_t = strength.T
        query_per_head = queries.transpose(1, 0, 2)
        key_per_head = key_rows.transpose(1, 0, 2)
        value_h = values.transpose(1, 0, 2)
        key_products = jnp.einsum('rxz,rfz->rxf', key_per_head, key_per_head, precision=highest_precision)
        spread = cumulative[:, :, None] - cumulative[:, None, :]
        decay_matrix = jnp.exp(jnp.where(inclusive_mask, spread, 0.0))
        lower = jnp.where(strict, strength_t[:, :, None] * decay_matrix * key_products, 0.0) + identity
        right_side = jnp.concatenate([(strength_t * growth)[..., None] * key_per_head, strength_t[..., None] * value_h], -1)
        solved = jax.scipy.linalg.solve_triangular(lower, right_side, lower=True, unit_diagonal=True)
        weights_w = solved[..., :DK]
        updates = solved[..., DK:]
        key_tail = tail[..., None] * key_per_head
        attention_scores = jnp.where(inclusive_mask, jnp.einsum('rxz,rfz->rxf', query_per_head, key_per_head, precision=highest_precision) * decay_matrix, 0.0)
        query_grown = growth[..., None] * query_per_head
        fresh = updates - jnp.einsum('hcd,hed->hce', weights_w, state, precision=highest_precision)
        read = jnp.einsum('hcd,hed->hce', query_grown, state, precision=highest_precision) + jnp.einsum('hcm,hme->hce', attention_scores, fresh, precision=highest_precision)
        new_state = jnp.exp(last_log)[..., None] * state + jnp.einsum('hce,hcd->hed', fresh, key_tail, precision=highest_precision)
        readout = narrowed(read).transpose(1, 0, 2)
        normed = readout * lax.rsqrt(lax.optimization_barrier(jnp.mean(readout * readout, -1, keepdims=True)) + 1e-06) * norm_gain
        return (new_state, normed.reshape(GROUP, HEADS * DV).astype(jnp.bfloat16))
    start = jnp.zeros((HEADS, DV, DK), jnp.float32)
    final_state, outputs = lax.scan(advance, start, blocks)
    return outputs.reshape(TOKENS, HEADS * DV)
```

```python
import functools

import jax
import jax.numpy as jnp
from jax import lax
from jax.experimental import pallas as pl
from jax.experimental.pallas import tpu as pltpu
from jax.sharding import PartitionSpec as P

HEADS = 16
DK = 128
DV = 128
CHUNK = 128
LANES = 128
F32 = jnp.float32
BF16 = jnp.bfloat16


def halves(a):
    high = a.astype(BF16)
    return high, (a - high.astype(F32)).astype(BF16)


def contract(a, b, dims):
    return lax.dot_general(a, b, dims, preferred_element_type=F32)


def dot3(a, b, ca, cb, batch=0):
    ah, al = halves(a)
    bh, bl = halves(b)
    lead = tuple(range(batch))
    dims = (((ca,), (cb,)), (lead, lead))
    return contract(ah, bh, dims) + (contract(ah, bl, dims) + contract(al, bh, dims))


def block_kernel(
    heads, x_ref, w_ref, wg_ref, rate_ref, bias_ref, read_ref, query_ref, state_ref, cum, cum_row, beta
):
    head = pl.program_id(0)
    rows = x_ref.shape[0]
    chunks = rows // CHUNK
    row_at = lax.broadcasted_iota(jnp.int32, (CHUNK, CHUNK), 0)
    col_at = lax.broadcasted_iota(jnp.int32, (CHUNK, CHUNK), 1)

    @pl.when(head == 0)
    def _():
        logits = contract(x_ref[...], wg_ref[...], (((1,), (0,)), ((), ())))
        soft = jnp.maximum(logits, 0.0) + jnp.log1p(jnp.exp(-jnp.abs(logits)))
        decay = (-rate_ref[...] * soft).astype(BF16)
        beta[...] = (
            (1.0 / (1.0 + jnp.exp(-(logits + bias_ref[...])))).astype(BF16).astype(F32)
        ).reshape(chunks, CHUNK, LANES)
        lower_ones = jnp.where(row_at >= col_at, 1.0, 0.0).astype(BF16)
        for c in range(chunks):
            piece = decay[c * CHUNK : (c + 1) * CHUNK]
            sums = contract(lower_ones, piece, (((1,), (0,)), ((), ())))
            cum[c] = sums
            cum_row[c] = sums.T

    raw = contract(x_ref[...], w_ref[0], (((1,), (0,)), ((), ())))
    raw_q = raw[:, :DK]
    raw_k = raw[:, DK : 2 * DK]
    q = (
        raw_q * lax.rsqrt(jnp.sum(raw_q * raw_q, -1, keepdims=True) + 1e-06) * DK ** (-0.5)
    ).astype(BF16)
    k = (raw_k * lax.rsqrt(jnp.sum(raw_k * raw_k, -1, keepdims=True) + 1e-06)).astype(BF16)
    v = raw[:, 2 * DK :].astype(BF16)
    q = q.reshape(chunks, CHUNK, DK)
    k = k.reshape(chunks, CHUNK, DK)
    v = v.reshape(chunks, CHUNK, DV).astype(F32)

    lane = lax.broadcasted_iota(jnp.int32, (chunks, CHUNK, LANES), 2)
    g = jnp.sum(jnp.where(lane == head, cum[...], 0.0), -1, keepdims=True)
    b = jnp.sum(jnp.where(lane == head + heads, beta[...], 0.0), -1, keepdims=True)
    g_row = cum_row[:, pl.ds(head, 1), :]
    g_last = g[:, CHUNK - 1 :, :]
    growth = jnp.exp(g)
    tail = jnp.exp(g_last - g)
    whole = jnp.exp(g_last)

    batched = (((2,), (2,)), ((0,), (0,)))
    pair = contract(jnp.concatenate([k, q], 1), k, batched)
    low = row_at >= col_at
    spread = jnp.exp(jnp.where(low[None], g - g_row, 0.0))
    lmat = jnp.where((row_at > col_at)[None], b * spread * pair[:, :CHUNK], 0.0)
    mmat = jnp.where(low[None], spread * pair[:, CHUNK:], 0.0)

    eye = jnp.where(row_at == col_at, 1.0, 0.0)
    inverse = None
    size = 1
    while size < CHUNK:
        inside = (row_at // (2 * size) == col_at // (2 * size)) & (row_at // size != col_at // size)
        off = jnp.where(inside[None], lmat, 0.0)
        if inverse is None:
            inverse = eye[None] - off
        else:
            inverse = inverse - dot3(inverse, dot3(off, inverse, 2, 1, 1), 2, 1, 1)
        size *= 2

    kf = k.astype(F32)
    right = jnp.concatenate([(b * growth) * kf, b * v], 2)
    wu = dot3(inverse, right, 2, 1, 1)
    mwu = dot3(mmat, wu, 2, 1, 1)
    moved = growth * q.astype(F32) - mwu[:, :, :DK]
    key_tail = tail * kf
    jumps = dot3(jnp.swapaxes(wu, 1, 2), key_tail, 2, 1, 1)
    step_map = whole * eye[None] - jumps[:, :DK]

    carry = jnp.concatenate([step_map[0], jumps[0, DK:]], 0)
    query_ref[:CHUNK] = moved[0]
    read_ref[:CHUNK] = mwu[0, :, DK:]
    for c in range(1, chunks):
        both = dot3(moved[c], carry, 1, 1)
        at = slice(c * CHUNK, (c + 1) * CHUNK)
        query_ref[at] = both[:, :DK]
        read_ref[at] = mwu[c, :, DK:] + both[:, DK:]
        carry = dot3(carry, step_map[c], 1, 0)
        carry = jnp.concatenate([carry[:DK], carry[DK:] + jumps[c, DK:]], 0)
    state_ref[0] = carry


def tail_kernel(place_ref, read_ref, query_ref, maps_ref, gain_ref, out_ref):
    def step(lap, state):
        return dot3(state, maps_ref[lap, 0, :DK, :], 1, 0) + maps_ref[lap, 0, DK:, :]

    state = lax.fori_loop(0, place_ref[0], step, jnp.zeros((DV, DK), F32))
    read = read_ref[...] + dot3(query_ref[...], state, 1, 1)
    readout = read.astype(BF16).astype(F32)
    scale = lax.rsqrt(jnp.mean(readout * readout, -1, keepdims=True) + 1e-06)
    out_ref[...] = (readout * scale * gain_ref[...]).astype(BF16)


def shards(
    tokens, w_query, w_key, w_value, decay_proj, beta_proj, decay_rate, beta_bias, norm_gain
):
    streams = lax.axis_size("stream")
    places = lax.axis_size("tm")
    heads = HEADS // streams
    depth = w_query.shape[0]
    share = depth // places
    place = lax.axis_index("tm")
    stream = lax.axis_index("stream")

    def mine(w):
        return lax.dynamic_slice_in_dim(w, place * share, share, 0)

    pieces = jnp.stack(
        [mine(w).reshape(share, streams, heads, DK) for w in (w_query, w_key, w_value)], 3
    ).reshape(share, streams, heads * 3 * DK)
    gates = jnp.concatenate(
        [mine(w).reshape(share, streams, heads) for w in (decay_proj, beta_proj)], 2
    )
    gates = jnp.pad(gates, ((0, 0), (0, 0), (0, LANES - 2 * heads)))
    sent = jnp.concatenate([pieces, gates], 2).transpose(1, 0, 2)
    swapped = lax.all_to_all(sent, "stream", 0, 0, tiled=True)
    full = lax.all_gather(swapped, "tm", axis=0)
    full = full.transpose(1, 0, 2, 3).reshape(streams * depth, -1)
    w_heads = full[:, : heads * 3 * DK].reshape(streams * depth, heads, 3 * DK).transpose(1, 0, 2)
    w_gates = full[:, heads * 3 * DK :]
    x = lax.all_gather(tokens, "stream", axis=0, tiled=True)
    rows = x.shape[0]
    width = x.shape[1]

    rate = lax.dynamic_slice_in_dim(decay_rate, stream * heads, heads)
    bias = lax.dynamic_slice_in_dim(beta_bias, stream * heads, heads)
    rate = jnp.pad(rate, (0, LANES - heads))[None]
    bias = jnp.pad(bias, (heads, LANES - 2 * heads))[None]

    chunks = rows // CHUNK
    read, moved, maps = pl.pallas_call(
        functools.partial(block_kernel, heads),
        grid=(heads,),
        out_shape=(
            jax.ShapeDtypeStruct((rows, heads * DV), F32),
            jax.ShapeDtypeStruct((rows, heads * DK), F32),
            jax.ShapeDtypeStruct((heads, DK + DV, DK), F32),
        ),
        in_specs=[
            pl.BlockSpec((rows, width), lambda h: (0, 0)),
            pl.BlockSpec((1, width, 3 * DK), lambda h: (h, 0, 0)),
            pl.BlockSpec((width, LANES), lambda h: (0, 0)),
            pl.BlockSpec((1, LANES), lambda h: (0, 0)),
            pl.BlockSpec((1, LANES), lambda h: (0, 0)),
        ],
        out_specs=(
            pl.BlockSpec((rows, DV), lambda h: (0, h)),
            pl.BlockSpec((rows, DK), lambda h: (0, h)),
            pl.BlockSpec((1, DK + DV, DK), lambda h: (h, 0, 0)),
        ),
        scratch_shapes=[
            pltpu.VMEM((chunks, CHUNK, LANES), F32),
            pltpu.VMEM((chunks, LANES, CHUNK), F32),
            pltpu.VMEM((chunks, CHUNK, LANES), F32),
        ],
    )(x, w_heads, w_gates, rate, bias)

    gathered = lax.all_gather(maps, "tm", axis=0)
    mixed = pl.pallas_call(
        tail_kernel,
        grid=(heads,),
        out_shape=jax.ShapeDtypeStruct((rows, heads * DV), BF16),
        in_specs=[
            pl.BlockSpec(memory_space=pltpu.SMEM),
            pl.BlockSpec((rows, DV), lambda h: (0, h)),
            pl.BlockSpec((rows, DK), lambda h: (0, h)),
            pl.BlockSpec((places, 1, DK + DV, DK), lambda h: (0, h, 0, 0)),
            pl.BlockSpec((1, DV), lambda h: (0, 0)),
        ],
        out_specs=pl.BlockSpec((rows, DV), lambda h: (0, h)),
    )(place[None].astype(jnp.int32), read, moved, gathered, norm_gain[None])
    return lax.all_to_all(mixed, "stream", split_axis=0, concat_axis=1, tiled=True)


def solution(mesh):
    return jax.shard_map(
        shards,
        mesh=mesh,
        in_specs=(
            P(("tm", "stream"), None),
            P("stream", None),
            P("stream", None),
            P("stream", None),
            P("stream", None),
            P("stream", None),
            P(),
            P(),
            P(),
        ),
        out_specs=P(("tm", "stream"), None),
        check_vma=False,
    )
```

```python
import functools

import jax
import jax.numpy as jnp
from jax import lax
from jax.experimental import pallas as pl
from jax.experimental.pallas import tpu as pltpu
from jax.sharding import PartitionSpec as P

HEADS = 16
DK = 128
DV = 128
CHUNK = 128
LANES = 128
F32 = jnp.float32
BF16 = jnp.bfloat16


def halves(a):
    high = a.astype(BF16)
    return high, (a - high.astype(F32)).astype(BF16)


def contract(a, b, dims):
    return lax.dot_general(a, b, dims, preferred_element_type=F32)


def dot3(a, b, ca, cb, batch=0):
    ah, al = halves(a)
    bh, bl = halves(b)
    lead = tuple(range(batch))
    dims = (((ca,), (cb,)), (lead, lead))
    return contract(ah, bh, dims) + (contract(ah, bl, dims) + contract(al, bh, dims))


def around(count):
    return sorted(range(1, count), key=lambda i: min(i, count - i))


def gather_kernel(
    streams,
    places,
    heads,
    tok_ref,
    wq_ref,
    wk_ref,
    wv_ref,
    wg_ref,
    x_ref,
    full_ref,
    stage,
    load_sem,
    own_sem,
    tok_recv,
    right_sem,
    left_sem,
    cross_send,
    cross_recv,
    plane_send,
    pass_send,
    plane_recv,
):
    t = lax.axis_index("tm")
    z = lax.axis_index("stream")
    chips = places // 2
    chip = t // 2
    core = t % 2
    group = heads * DK

    loads = []
    for dest in range(streams):
        for j, ref in enumerate((wq_ref, wk_ref, wv_ref)):
            loads.append(
                pltpu.make_async_copy(
                    ref.at[t, :, pl.ds(dest * group, group)],
                    stage.at[dest, :, pl.ds(j * group, group)],
                    load_sem.at[dest, j],
                )
            )
        loads.append(
            pltpu.make_async_copy(
                wg_ref.at[t], stage.at[dest, :, pl.ds(3 * group, LANES)], load_sem.at[dest, 3]
            )
        )
    for copy in loads:
        copy.start()

    others = [(lax.rem(chip + i, chips) * 2 + core) for i in range(1, chips)]
    sibling = chip * 2 + 1 - core
    peers = [(t, lax.rem(z + i, streams)) for i in around(streams)]
    peers += [(sibling, z)] + [(o, z) for o in others]
    barrier = pltpu.get_barrier_semaphore()
    for peer in peers:
        pl.semaphore_signal(
            barrier, inc=1, device_id=peer, device_id_type=pl.DeviceIdType.MESH
        )
    pl.semaphore_wait(barrier, len(peers))
    for copy in loads:
        copy.wait()

    def remote(src, dst, send, recv, device):
        return pltpu.make_async_remote_copy(
            src_ref=src,
            dst_ref=dst,
            send_sem=send,
            recv_sem=recv,
            device_id=device,
            device_id_type=pl.DeviceIdType.MESH,
        )

    def cross(i):
        dest = lax.rem(z + i, streams)
        return remote(
            stage.at[dest], full_ref.at[t, z], cross_send.at[dest], cross_recv.at[z], (t, dest)
        )

    def crossed(i):
        s = lax.rem(z + i, streams)
        return remote(
            stage.at[s], full_ref.at[t, s], cross_send.at[s], cross_recv.at[s], (t, s)
        )

    def line(chunk, right, first):
        src = tok_ref if first else x_ref.at[chunk]
        send = (right_sem if right else left_sem).at[chunk]
        return remote(
            src, x_ref.at[chunk], send, tok_recv.at[chunk], (t, z + 1 if right else z - 1)
        )

    def plane(i, s, first):
        to = sibling if i == 0 else others[i - 1]
        src = stage.at[z] if first else full_ref.at[t, s]
        return remote(
            src, full_ref.at[t, s], plane_send.at[i, s], plane_recv.at[t, s], (to, z)
        )

    def relay(i, s):
        at = others[i - 1]
        here = full_ref.at[at, s]
        return remote(here, here, pass_send.at[i, s], plane_recv.at[at, s], (sibling, z))

    def landed(at, s):
        here = full_ref.at[at, s]
        return remote(here, here, plane_send.at[0, s], plane_recv.at[at, s], (sibling, z))

    for i in around(streams):
        cross(i).start()

    @pl.when(z < streams - 1)
    def _():
        line(z, True, True).start()

    @pl.when(z > 0)
    def _():
        line(z, False, True).start()

    for i in range(1, chips):
        plane(i, z, True).start()
    plane(0, z, True).start()
    own = [
        pltpu.make_async_copy(stage.at[z], full_ref.at[t, z], own_sem.at[0]),
        pltpu.make_async_copy(tok_ref, x_ref.at[z], own_sem.at[1]),
    ]
    for copy in own:
        copy.start()

    for i in around(streams):
        s = lax.rem(z + i, streams)
        crossed(i).wait_recv()
        for j in range(1, chips):
            plane(j, s, False).start()
        plane(0, s, False).start()

    def step(k):
        @pl.when(z >= k)
        def _():
            line(z - k, True, False).wait_recv()

            @pl.when(z < streams - 1)
            def _():
                line(z - k, True, False).start()

        @pl.when(z + k < streams)
        def _():
            line(z + k, False, False).wait_recv()

            @pl.when(z > 0)
            def _():
                line(z + k, False, False).start()

    orders = [z] + [lax.rem(z + i, streams) for i in around(streams)]
    passed = 0
    for k in range(1, streams):
        step(k)
        upto = len(orders) if k == streams - 2 else passed + 1
        while passed < min(upto, len(orders)):
            s = orders[passed]
            for i in range(1, chips):
                landed(others[i - 1], s).wait_recv()
                relay(i, s).start()
            passed += 1
    while passed < len(orders):
        s = orders[passed]
        for i in range(1, chips):
            landed(others[i - 1], s).wait_recv()
            relay(i, s).start()
        passed += 1

    for copy in own:
        copy.wait()
    for s in orders:
        landed(sibling, s).wait_recv()
        for i in range(1, chips):
            landed(lax.rem(chip + i, chips) * 2 + 1 - core, s).wait_recv()
    for i in around(streams):
        cross(i).wait_send()
    for n, s in enumerate(orders):
        for i in range(chips):
            plane(i, s, n == 0).wait_send()
        for i in range(1, chips):
            relay(i, s).wait_send()
    for k in range(streams):

        @pl.when((z >= k) & (z < streams - 1))
        def _():
            line(z - k, True, k == 0).wait_send()

        @pl.when((z + k < streams) & (z > 0))
        def _():
            line(z + k, False, k == 0).wait_send()


def block_kernel(
    heads,
    x_ref,
    wq_ref,
    wk_ref,
    wv_ref,
    wg_ref,
    rate_ref,
    bias_ref,
    read_ref,
    query_ref,
    state_ref,
    cum,
    cum_row,
    beta,
):
    first_head = lax.axis_index("stream") * heads
    head = pl.program_id(0) + first_head
    rows = x_ref.shape[0]
    places, streams, share, _ = wq_ref.shape
    depth = places * share

    def project(refs):
        total = None
        for s in range(streams):
            w = jnp.concatenate([ref[:, s].reshape(depth, LANES) for ref in refs], 1)
            term = contract(x_ref[:, s * depth : (s + 1) * depth], w, (((1,), (0,)), ((), ())))
            total = term if total is None else total + term
        return total

    chunks = rows // CHUNK
    row_at = lax.broadcasted_iota(jnp.int32, (CHUNK, CHUNK), 0)
    col_at = lax.broadcasted_iota(jnp.int32, (CHUNK, CHUNK), 1)

    @pl.when(pl.program_id(0) == 0)
    def _():
        logits = project((wg_ref,))
        soft = jnp.maximum(logits, 0.0) + jnp.log1p(jnp.exp(-jnp.abs(logits)))
        decay = (-rate_ref[...] * soft).astype(BF16)
        beta[...] = (
            (1.0 / (1.0 + jnp.exp(-(logits + bias_ref[...])))).astype(BF16).astype(F32)
        ).reshape(chunks, CHUNK, LANES)
        lower_ones = jnp.where(row_at >= col_at, 1.0, 0.0).astype(BF16)
        for c in range(chunks):
            piece = decay[c * CHUNK : (c + 1) * CHUNK]
            sums = contract(lower_ones, piece, (((1,), (0,)), ((), ())))
            cum[c] = sums
            cum_row[c] = sums.T

    raw = project((wq_ref, wk_ref, wv_ref))
    raw_q = raw[:, :DK]
    raw_k = raw[:, DK : 2 * DK]
    q = (
        raw_q * lax.rsqrt(jnp.sum(raw_q * raw_q, -1, keepdims=True) + 1e-06) * DK ** (-0.5)
    ).astype(BF16)
    k = (raw_k * lax.rsqrt(jnp.sum(raw_k * raw_k, -1, keepdims=True) + 1e-06)).astype(BF16)
    v = raw[:, 2 * DK :].astype(BF16)
    q = q.reshape(chunks, CHUNK, DK)
    k = k.reshape(chunks, CHUNK, DK)
    v = v.reshape(chunks, CHUNK, DV).astype(F32)

    lane = lax.broadcasted_iota(jnp.int32, (chunks, CHUNK, LANES), 2)
    g = jnp.sum(jnp.where(lane == head, cum[...], 0.0), -1, keepdims=True)
    b = jnp.sum(jnp.where(lane == head + HEADS, beta[...], 0.0), -1, keepdims=True)
    g_row = cum_row[:, pl.ds(head, 1), :]
    g_last = g[:, CHUNK - 1 :, :]
    growth = jnp.exp(g)
    tail = jnp.exp(g_last - g)
    whole = jnp.exp(g_last)

    batched = (((2,), (2,)), ((0,), (0,)))
    pair = contract(jnp.concatenate([k, q], 1), k, batched)
    low = row_at >= col_at
    spread = jnp.exp(jnp.where(low[None], g - g_row, 0.0))
    lmat = jnp.where((row_at > col_at)[None], b * spread * pair[:, :CHUNK], 0.0)
    mmat = jnp.where(low[None], spread * pair[:, CHUNK:], 0.0)

    eye = jnp.where(row_at == col_at, 1.0, 0.0)
    inverse = None
    size = 1
    while size < CHUNK:
        inside = (row_at // (2 * size) == col_at // (2 * size)) & (row_at // size != col_at // size)
        off = jnp.where(inside[None], lmat, 0.0)
        if inverse is None:
            inverse = eye[None] - off
        else:
            inverse = inverse - dot3(inverse, dot3(off, inverse, 2, 1, 1), 2, 1, 1)
        size *= 2

    kf = k.astype(F32)
    right = jnp.concatenate([(b * growth) * kf, b * v], 2)
    wu = dot3(inverse, right, 2, 1, 1)
    mwu = dot3(mmat, wu, 2, 1, 1)
    moved = growth * q.astype(F32) - mwu[:, :, :DK]
    key_tail = tail * kf
    jumps = dot3(jnp.swapaxes(wu, 1, 2), key_tail, 2, 1, 1)
    step_map = whole * eye[None] - jumps[:, :DK]

    carry = jnp.concatenate([step_map[0], jumps[0, DK:]], 0)
    query_ref[:CHUNK] = moved[0]
    read_ref[:CHUNK] = mwu[0, :, DK:]
    for c in range(1, chunks):
        both = dot3(moved[c], carry, 1, 1)
        at = slice(c * CHUNK, (c + 1) * CHUNK)
        query_ref[at] = both[:, :DK]
        read_ref[at] = mwu[c, :, DK:] + both[:, DK:]
        carry = dot3(carry, step_map[c], 1, 0)
        carry = jnp.concatenate([carry[:DK], carry[DK:] + jumps[c, DK:]], 0)
    state_ref[0] = carry


def tail_kernel(place_ref, read_ref, query_ref, maps_ref, gain_ref, out_ref):
    def step(lap, state):
        return dot3(state, maps_ref[lap, 0, :DK, :], 1, 0) + maps_ref[lap, 0, DK:, :]

    state = lax.fori_loop(0, place_ref[0], step, jnp.zeros((DV, DK), F32))
    read = read_ref[...] + dot3(query_ref[...], state, 1, 1)
    readout = read.astype(BF16).astype(F32)
    scale = lax.rsqrt(jnp.mean(readout * readout, -1, keepdims=True) + 1e-06)
    out_ref[...] = (readout * scale * gain_ref[...]).astype(BF16)


def shards(
    tokens, w_query, w_key, w_value, decay_proj, beta_proj, decay_rate, beta_bias, norm_gain
):
    streams = lax.axis_size("stream")
    places = lax.axis_size("tm")
    heads = HEADS // streams
    depth = w_query.shape[0]
    share = depth // places
    place = lax.axis_index("tm")
    width = 3 * heads * DK + LANES
    gates = jnp.pad(
        jnp.concatenate([decay_proj, beta_proj], 1), ((0, 0), (0, LANES - 2 * HEADS))
    )
    shares = [w.reshape(places, share, -1) for w in (w_query, w_key, w_value, gates)]
    local, features = tokens.shape
    any_space = pl.BlockSpec(memory_space=pl.ANY)
    dma = pltpu.SemaphoreType.DMA
    chips = places // 2
    x, full = pl.pallas_call(
        functools.partial(gather_kernel, streams, places, heads),
        out_shape=(
            jax.ShapeDtypeStruct((streams, local, features), BF16),
            jax.ShapeDtypeStruct((places, streams, share, width), BF16),
        ),
        in_specs=[pl.BlockSpec(memory_space=pltpu.VMEM)] + [any_space] * 4,
        out_specs=(any_space, any_space),
        scratch_shapes=[
            pltpu.VMEM((streams, share, width), BF16),
            dma((streams, 4)),
            dma((2,)),
            dma((streams,)),
            dma((streams,)),
            dma((streams,)),
            dma((streams,)),
            dma((streams,)),
            dma((chips, streams)),
            dma((chips, streams)),
            dma((places, streams)),
        ],
        compiler_params=pltpu.CompilerParams(collective_id=0, has_side_effects=True),
    )(tokens, *shares)
    x = x.reshape(streams * local, features)
    rows = x.shape[0]
    if share % 16:
        full = full.transpose(1, 0, 2, 3).reshape(1, streams, places * share, width)

    rate = jnp.pad(decay_rate, (0, LANES - HEADS))[None]
    bias = jnp.pad(beta_bias, (HEADS, LANES - 2 * HEADS))[None]

    chunks = rows // CHUNK
    read, moved, maps = pl.pallas_call(
        functools.partial(block_kernel, heads),
        grid=(heads,),
        out_shape=(
            jax.ShapeDtypeStruct((rows, heads * DV), F32),
            jax.ShapeDtypeStruct((rows, heads * DK), F32),
            jax.ShapeDtypeStruct((heads, DK + DV, DK), F32),
        ),
        in_specs=[
            pl.BlockSpec((rows, features), lambda h: (0, 0)),
            pl.BlockSpec(full.shape[:3] + (DK,), lambda h: (0, 0, 0, h)),
            pl.BlockSpec(full.shape[:3] + (DK,), lambda h: (0, 0, 0, heads + h)),
            pl.BlockSpec(full.shape[:3] + (DV,), lambda h: (0, 0, 0, 2 * heads + h)),
            pl.BlockSpec(full.shape[:3] + (LANES,), lambda h: (0, 0, 0, 3 * heads)),
            pl.BlockSpec((1, LANES), lambda h: (0, 0)),
            pl.BlockSpec((1, LANES), lambda h: (0, 0)),
        ],
        out_specs=(
            pl.BlockSpec((rows, DV), lambda h: (0, h)),
            pl.BlockSpec((rows, DK), lambda h: (0, h)),
            pl.BlockSpec((1, DK + DV, DK), lambda h: (h, 0, 0)),
        ),
        scratch_shapes=[
            pltpu.VMEM((chunks, CHUNK, LANES), F32),
            pltpu.VMEM((chunks, LANES, CHUNK), F32),
            pltpu.VMEM((chunks, CHUNK, LANES), F32),
        ],
    )(x, full, full, full, full, rate, bias)

    gathered = lax.all_gather(maps, "tm", axis=0)
    mixed = pl.pallas_call(
        tail_kernel,
        grid=(heads,),
        out_shape=jax.ShapeDtypeStruct((rows, heads * DV), BF16),
        in_specs=[
            pl.BlockSpec(memory_space=pltpu.SMEM),
            pl.BlockSpec((rows, DV), lambda h: (0, h)),
            pl.BlockSpec((rows, DK), lambda h: (0, h)),
            pl.BlockSpec((places, 1, DK + DV, DK), lambda h: (0, h, 0, 0)),
            pl.BlockSpec((1, DV), lambda h: (0, 0)),
        ],
        out_specs=pl.BlockSpec((rows, DV), lambda h: (0, h)),
    )(place[None].astype(jnp.int32), read, moved, gathered, norm_gain[None])
    return lax.all_to_all(mixed, "stream", split_axis=0, concat_axis=1, tiled=True)


def solution(mesh):
    return jax.shard_map(
        shards,
        mesh=mesh,
        in_specs=(
            P(("tm", "stream"), None),
            P("stream", None),
            P("stream", None),
            P("stream", None),
            P("stream", None),
            P("stream", None),
            P(),
            P(),
            P(),
        ),
        out_specs=P(("tm", "stream"), None),
        check_vma=False,
    )
```

```python
import functools

import jax
import jax.numpy as jnp
from jax import lax
from jax.experimental import pallas as pl
from jax.experimental.pallas import tpu as pltpu
from jax.sharding import PartitionSpec as P

HEADS = 16
DK = 128
DV = 128
CHUNK = 128
LANES = 128
F32 = jnp.float32
BF16 = jnp.bfloat16


def halves(a):
    high = a.astype(BF16)
    return high, (a - high.astype(F32)).astype(BF16)


def contract(a, b, dims):
    return lax.dot_general(a, b, dims, preferred_element_type=F32)


def dot3(a, b, ca, cb, batch=0):
    ah, al = halves(a)
    bh, bl = halves(b)
    lead = tuple(range(batch))
    dims = (((ca,), (cb,)), (lead, lead))
    return contract(ah, bh, dims) + (contract(ah, bl, dims) + contract(al, bh, dims))


def around(count):
    return sorted(range(1, count), key=lambda i: min(i, count - i))


def gather_kernel(
    streams,
    places,
    heads,
    tok_ref,
    wq_ref,
    wk_ref,
    wv_ref,
    wg_ref,
    x_ref,
    full_ref,
    stage,
    load_sem,
    own_sem,
    tok_recv,
    right_sem,
    left_sem,
    cross_send,
    cross_recv,
    plane_send,
    pass_send,
    plane_recv,
):
    t = lax.axis_index("tm")
    z = lax.axis_index("stream")
    chips = places // 2
    chip = t // 2
    core = t % 2
    group = heads * DK

    loads = []
    for dest in range(streams):
        for j, ref in enumerate((wq_ref, wk_ref, wv_ref)):
            loads.append(
                pltpu.make_async_copy(
                    ref.at[t, :, pl.ds(dest * group, group)],
                    stage.at[dest, :, pl.ds(j * group, group)],
                    load_sem.at[dest, j],
                )
            )
        loads.append(
            pltpu.make_async_copy(
                wg_ref.at[t], stage.at[dest, :, pl.ds(3 * group, LANES)], load_sem.at[dest, 3]
            )
        )
    for copy in loads:
        copy.start()

    others = [(lax.rem(chip + i, chips) * 2 + core) for i in range(1, chips)]
    sibling = chip * 2 + 1 - core
    peers = [(t, lax.rem(z + i, streams)) for i in around(streams)]
    peers += [(sibling, z)] + [(o, z) for o in others]
    barrier = pltpu.get_barrier_semaphore()
    for peer in peers:
        pl.semaphore_signal(
            barrier, inc=1, device_id=peer, device_id_type=pl.DeviceIdType.MESH
        )
    pl.semaphore_wait(barrier, len(peers))
    for copy in loads:
        copy.wait()

    def remote(src, dst, send, recv, device):
        return pltpu.make_async_remote_copy(
            src_ref=src,
            dst_ref=dst,
            send_sem=send,
            recv_sem=recv,
            device_id=device,
            device_id_type=pl.DeviceIdType.MESH,
        )

    def cross(i):
        dest = lax.rem(z + i, streams)
        return remote(
            stage.at[dest], full_ref.at[t, z], cross_send.at[dest], cross_recv.at[z], (t, dest)
        )

    def crossed(i):
        s = lax.rem(z + i, streams)
        return remote(
            stage.at[s], full_ref.at[t, s], cross_send.at[s], cross_recv.at[s], (t, s)
        )

    def line(chunk, right, first):
        src = tok_ref if first else x_ref.at[chunk]
        send = (right_sem if right else left_sem).at[chunk]
        return remote(
            src, x_ref.at[chunk], send, tok_recv.at[chunk], (t, z + 1 if right else z - 1)
        )

    def plane(i, s, first):
        to = sibling if i == 0 else others[i - 1]
        src = stage.at[z] if first else full_ref.at[t, s]
        return remote(
            src, full_ref.at[t, s], plane_send.at[i, s], plane_recv.at[t, s], (to, z)
        )

    def relay(i, s):
        at = others[i - 1]
        here = full_ref.at[at, s]
        return remote(here, here, pass_send.at[i, s], plane_recv.at[at, s], (sibling, z))

    def landed(at, s):
        here = full_ref.at[at, s]
        return remote(here, here, plane_send.at[0, s], plane_recv.at[at, s], (sibling, z))

    for i in around(streams):
        cross(i).start()

    @pl.when(z < streams - 1)
    def _():
        line(z, True, True).start()

    @pl.when(z > 0)
    def _():
        line(z, False, True).start()

    for i in range(1, chips):
        plane(i, z, True).start()
    plane(0, z, True).start()
    own = [
        pltpu.make_async_copy(stage.at[z], full_ref.at[t, z], own_sem.at[0]),
        pltpu.make_async_copy(tok_ref, x_ref.at[z], own_sem.at[1]),
    ]
    for copy in own:
        copy.start()

    for i in around(streams):
        s = lax.rem(z + i, streams)
        crossed(i).wait_recv()
        for j in range(1, chips):
            plane(j, s, False).start()
        plane(0, s, False).start()

    def step(k):
        @pl.when(z >= k)
        def _():
            line(z - k, True, False).wait_recv()

            @pl.when(z < streams - 1)
            def _():
                line(z - k, True, False).start()

        @pl.when(z + k < streams)
        def _():
            line(z + k, False, False).wait_recv()

            @pl.when(z > 0)
            def _():
                line(z + k, False, False).start()

    orders = [z] + [lax.rem(z + i, streams) for i in around(streams)]
    passed = 0
    for k in range(1, streams):
        step(k)
        upto = len(orders) if k == streams - 2 else passed + 1
        while passed < min(upto, len(orders)):
            s = orders[passed]
            for i in range(1, chips):
                landed(others[i - 1], s).wait_recv()
                relay(i, s).start()
            passed += 1
    while passed < len(orders):
        s = orders[passed]
        for i in range(1, chips):
            landed(others[i - 1], s).wait_recv()
            relay(i, s).start()
        passed += 1

    for copy in own:
        copy.wait()
    for s in orders:
        landed(sibling, s).wait_recv()
        for i in range(1, chips):
            landed(lax.rem(chip + i, chips) * 2 + 1 - core, s).wait_recv()
    for i in around(streams):
        cross(i).wait_send()
    for n, s in enumerate(orders):
        for i in range(chips):
            plane(i, s, n == 0).wait_send()
        for i in range(1, chips):
            relay(i, s).wait_send()
    for k in range(streams):

        @pl.when((z >= k) & (z < streams - 1))
        def _():
            line(z - k, True, k == 0).wait_send()

        @pl.when((z + k < streams) & (z > 0))
        def _():
            line(z + k, False, k == 0).wait_send()


def block_kernel(
    heads,
    x_ref,
    wq_ref,
    wk_ref,
    wv_ref,
    wg_ref,
    rate_ref,
    bias_ref,
    read_ref,
    query_ref,
    state_ref,
    cum,
    cum_row,
    beta,
):
    first_head = lax.axis_index("stream") * heads
    head = pl.program_id(0) + first_head
    rows = x_ref.shape[0]
    places, streams, share, _ = wq_ref.shape
    depth = places * share

    def project(refs):
        total = None
        for s in range(streams):
            w = jnp.concatenate([ref[:, s].reshape(depth, LANES) for ref in refs], 1)
            term = contract(x_ref[:, s * depth : (s + 1) * depth], w, (((1,), (0,)), ((), ())))
            total = term if total is None else total + term
        return total

    chunks = rows // CHUNK
    row_at = lax.broadcasted_iota(jnp.int32, (CHUNK, CHUNK), 0)
    col_at = lax.broadcasted_iota(jnp.int32, (CHUNK, CHUNK), 1)

    @pl.when(pl.program_id(0) == 0)
    def _():
        logits = project((wg_ref,))
        soft = jnp.maximum(logits, 0.0) + jnp.log1p(jnp.exp(-jnp.abs(logits)))
        decay = (-rate_ref[...] * soft).astype(BF16)
        beta[...] = (
            (1.0 / (1.0 + jnp.exp(-(logits + bias_ref[...])))).astype(BF16).astype(F32)
        ).reshape(chunks, CHUNK, LANES)
        lower_ones = jnp.where(row_at >= col_at, 1.0, 0.0).astype(BF16)
        for c in range(chunks):
            piece = decay[c * CHUNK : (c + 1) * CHUNK]
            sums = contract(lower_ones, piece, (((1,), (0,)), ((), ())))
            cum[c] = sums
            cum_row[c] = sums.T

    raw = project((wq_ref, wk_ref, wv_ref))
    raw_q = raw[:, :DK]
    raw_k = raw[:, DK : 2 * DK]
    q = (
        raw_q * lax.rsqrt(jnp.sum(raw_q * raw_q, -1, keepdims=True) + 1e-06) * DK ** (-0.5)
    ).astype(BF16)
    k = (raw_k * lax.rsqrt(jnp.sum(raw_k * raw_k, -1, keepdims=True) + 1e-06)).astype(BF16)
    v = raw[:, 2 * DK :].astype(BF16)
    q = q.reshape(chunks, CHUNK, DK)
    k = k.reshape(chunks, CHUNK, DK)
    v = v.reshape(chunks, CHUNK, DV).astype(F32)

    lane = lax.broadcasted_iota(jnp.int32, (chunks, CHUNK, LANES), 2)
    g = jnp.sum(jnp.where(lane == head, cum[...], 0.0), -1, keepdims=True)
    b = jnp.sum(jnp.where(lane == head + HEADS, beta[...], 0.0), -1, keepdims=True)
    g_row = cum_row[:, pl.ds(head, 1), :]
    g_last = g[:, CHUNK - 1 :, :]
    growth = jnp.exp(g)
    tail = jnp.exp(g_last - g)
    whole = jnp.exp(g_last)

    batched = (((2,), (2,)), ((0,), (0,)))
    pair = contract(jnp.concatenate([k, q], 1), k, batched)
    low = row_at >= col_at
    spread = jnp.exp(jnp.where(low[None], g - g_row, 0.0))
    lmat = jnp.where((row_at > col_at)[None], b * spread * pair[:, :CHUNK], 0.0)
    mmat = jnp.where(low[None], spread * pair[:, CHUNK:], 0.0)

    eye = jnp.where(row_at == col_at, 1.0, 0.0)
    inverse = None
    size = 1
    while size < CHUNK:
        inside = (row_at // (2 * size) == col_at // (2 * size)) & (row_at // size != col_at // size)
        off = jnp.where(inside[None], lmat, 0.0)
        if inverse is None:
            inverse = eye[None] - off
        else:
            inverse = inverse - dot3(inverse, dot3(off, inverse, 2, 1, 1), 2, 1, 1)
        size *= 2

    kf = k.astype(F32)
    right = jnp.concatenate([(b * growth) * kf, b * v], 2)
    wu = dot3(inverse, right, 2, 1, 1)
    mwu = dot3(mmat, wu, 2, 1, 1)
    moved = growth * q.astype(F32) - mwu[:, :, :DK]
    key_tail = tail * kf
    jumps = dot3(jnp.swapaxes(wu, 1, 2), key_tail, 2, 1, 1)
    step_map = whole * eye[None] - jumps[:, :DK]

    carry = jnp.concatenate([step_map[0], jumps[0, DK:]], 0)
    query_ref[:CHUNK] = moved[0]
    read_ref[:CHUNK] = mwu[0, :, DK:]
    for c in range(1, chunks):
        both = dot3(moved[c], carry, 1, 1)
        at = slice(c * CHUNK, (c + 1) * CHUNK)
        query_ref[at] = both[:, :DK]
        read_ref[at] = mwu[c, :, DK:] + both[:, DK:]
        carry = dot3(carry, step_map[c], 1, 0)
        carry = jnp.concatenate([carry[:DK], carry[DK:] + jumps[c, DK:]], 0)
    state_ref[0] = carry


def return_kernel(
    streams,
    places,
    heads,
    read_ref,
    query_ref,
    maps_ref,
    gain_ref,
    out_ref,
    pair,
    total,
    got,
    carried,
    state,
    mixed,
    pair_sem,
    state_sem,
    chip_send,
    chip_recv,
    out_send,
    out_recv,
    own_sem,
):
    t = lax.axis_index("tm")
    z = lax.axis_index("stream")
    chips = places // 2
    chip = t // 2
    core = t % 2
    sibling = chip * 2 + 1 - core
    group = heads * DV
    local = out_ref.shape[0]

    peers = [(t, lax.rem(z + i, streams)) for i in around(streams)]
    peers += [(sibling, z)]
    peers += [(lax.rem(chip + i, chips) * 2 + core, z) for i in range(1, chips)]
    barrier = pltpu.get_barrier_semaphore()
    for peer in peers:
        pl.semaphore_signal(
            barrier, inc=1, device_id=peer, device_id_type=pl.DeviceIdType.MESH
        )
    pl.semaphore_wait(barrier, len(peers))

    def remote(src, dst, send, recv, device):
        return pltpu.make_async_remote_copy(
            src_ref=src,
            dst_ref=dst,
            send_sem=send,
            recv_sem=recv,
            device_id=device,
            device_id_type=pl.DeviceIdType.MESH,
        )

    def hand_over():
        return remote(maps_ref, pair, pair_sem.at[0], pair_sem.at[1], (sibling, z))

    def hand_back():
        return remote(carried, carried, state_sem.at[0], state_sem.at[1], (sibling, z))

    def to_chip(source, dest):
        src, dst = total, got.at[source]
        if source == 0:
            src, dst = total.at[:, pl.ds(DK, DV)], got.at[0, :, pl.ds(DK, DV)]
        return remote(src, dst, chip_send.at[dest], chip_recv.at[source], (dest * 2 + 1, z))

    @pl.when(core == 0)
    def _():
        hand_over().start()
        hand_over().wait_send()

    @pl.when(core == 1)
    def _():
        hand_over().wait_recv()

        @pl.when(chip < chips - 1)
        def _():
            for h in range(heads):
                both = dot3(pair[h], maps_ref[h, :DK], 1, 0)
                total[h, :DK] = both[:DK]
                total[h, DK:] = both[DK:] + maps_ref[h, DK:]

        for source in range(chips - 1):

            @pl.when(chip == source)
            def _():
                for dest in range(chips - 1, source, -1):
                    to_chip(source, dest).start()

        for source in range(chips - 1):

            @pl.when(chip > source)
            def _():
                to_chip(source, chip).wait_recv()
                for h in range(heads):
                    if source == 0:
                        carried[h] = got[0, h, DK:]
                    else:
                        carried[h] = dot3(carried[h], got[source, h, :DK], 1, 0) + got[source, h, DK:]

        @pl.when(chip > 0)
        def _():
            hand_back().start()
            for h in range(heads):
                state[h] = dot3(carried[h], pair[h, :DK], 1, 0) + pair[h, DK:]

        @pl.when(chip == 0)
        def _():
            for h in range(heads):
                state[h] = pair[h, DK:]

    @pl.when((core == 0) & (chip > 0))
    def _():
        hand_back().wait_recv()
        for h in range(heads):
            state[h] = carried[h]

    @pl.when((core == 0) & (chip == 0))
    def _():
        state[...] = jnp.zeros_like(state)

    def outgoing(i):
        dest = lax.rem(z + i, streams)
        dst = out_ref.at[:, pl.ds(pl.multiple_of(z * group, group), group)]
        return remote(mixed.at[dest], dst, out_send.at[dest], out_recv.at[z], (t, dest))

    def incoming(i):
        source = lax.rem(z + i, streams)
        dst = out_ref.at[:, pl.ds(pl.multiple_of(source * group, group), group)]
        return remote(mixed.at[source], dst, out_send.at[source], out_recv.at[source], (t, source))

    own = pltpu.make_async_copy(
        mixed.at[z], out_ref.at[:, pl.ds(pl.multiple_of(z * group, group), group)], own_sem.at[0]
    )
    order = list(reversed(around(streams)))
    for i in order + [0]:
        dest = lax.rem(z + i, streams)
        at = pl.ds(pl.multiple_of(dest * local, local), local)
        for h in range(heads):
            lanes = slice(h * DV, (h + 1) * DV)
            read = read_ref[at, lanes] + dot3(query_ref[at, lanes], state[h], 1, 1)
            readout = read.astype(BF16).astype(F32)
            scale = lax.rsqrt(jnp.mean(readout * readout, -1, keepdims=True) + 1e-06)
            mixed[dest, :, lanes] = (readout * scale * gain_ref[...]).astype(BF16)
        if i == 0:
            own.start()
        else:
            outgoing(i).start()

    own.wait()
    for i in order:
        incoming(i).wait_recv()
    for i in order:
        outgoing(i).wait_send()

    @pl.when((core == 1) & (chip > 0))
    def _():
        hand_back().wait_send()

    for source in range(chips - 1):

        @pl.when((core == 1) & (chip == source))
        def _():
            for dest in range(chips - 1, source, -1):
                to_chip(source, dest).wait_send()


def shards(
    tokens, w_query, w_key, w_value, decay_proj, beta_proj, decay_rate, beta_bias, norm_gain
):
    streams = lax.axis_size("stream")
    places = lax.axis_size("tm")
    heads = HEADS // streams
    depth = w_query.shape[0]
    share = depth // places
    width = 3 * heads * DK + LANES
    gates = jnp.pad(
        jnp.concatenate([decay_proj, beta_proj], 1), ((0, 0), (0, LANES - 2 * HEADS))
    )
    shares = [w.reshape(places, share, -1) for w in (w_query, w_key, w_value, gates)]
    local, features = tokens.shape
    any_space = pl.BlockSpec(memory_space=pl.ANY)
    dma = pltpu.SemaphoreType.DMA
    chips = places // 2
    x, full = pl.pallas_call(
        functools.partial(gather_kernel, streams, places, heads),
        out_shape=(
            jax.ShapeDtypeStruct((streams, local, features), BF16),
            jax.ShapeDtypeStruct((places, streams, share, width), BF16),
        ),
        in_specs=[pl.BlockSpec(memory_space=pltpu.VMEM)] + [any_space] * 4,
        out_specs=(any_space, any_space),
        scratch_shapes=[
            pltpu.VMEM((streams, share, width), BF16),
            dma((streams, 4)),
            dma((2,)),
            dma((streams,)),
            dma((streams,)),
            dma((streams,)),
            dma((streams,)),
            dma((streams,)),
            dma((chips, streams)),
            dma((chips, streams)),
            dma((places, streams)),
        ],
        compiler_params=pltpu.CompilerParams(collective_id=0, has_side_effects=True),
    )(tokens, *shares)
    x = x.reshape(streams * local, features)
    rows = x.shape[0]
    if share % 16:
        full = full.transpose(1, 0, 2, 3).reshape(1, streams, places * share, width)

    rate = jnp.pad(decay_rate, (0, LANES - HEADS))[None]
    bias = jnp.pad(beta_bias, (HEADS, LANES - 2 * HEADS))[None]

    chunks = rows // CHUNK
    read, moved, maps = pl.pallas_call(
        functools.partial(block_kernel, heads),
        grid=(heads,),
        out_shape=(
            jax.ShapeDtypeStruct((rows, heads * DV), F32),
            jax.ShapeDtypeStruct((rows, heads * DK), F32),
            jax.ShapeDtypeStruct((heads, DK + DV, DK), F32),
        ),
        in_specs=[
            pl.BlockSpec((rows, features), lambda h: (0, 0)),
            pl.BlockSpec(full.shape[:3] + (DK,), lambda h: (0, 0, 0, h)),
            pl.BlockSpec(full.shape[:3] + (DK,), lambda h: (0, 0, 0, heads + h)),
            pl.BlockSpec(full.shape[:3] + (DV,), lambda h: (0, 0, 0, 2 * heads + h)),
            pl.BlockSpec(full.shape[:3] + (LANES,), lambda h: (0, 0, 0, 3 * heads)),
            pl.BlockSpec((1, LANES), lambda h: (0, 0)),
            pl.BlockSpec((1, LANES), lambda h: (0, 0)),
        ],
        out_specs=(
            pl.BlockSpec((rows, DV), lambda h: (0, h)),
            pl.BlockSpec((rows, DK), lambda h: (0, h)),
            pl.BlockSpec((1, DK + DV, DK), lambda h: (h, 0, 0)),
        ),
        scratch_shapes=[
            pltpu.VMEM((chunks, CHUNK, LANES), F32),
            pltpu.VMEM((chunks, LANES, CHUNK), F32),
            pltpu.VMEM((chunks, CHUNK, LANES), F32),
        ],
    )(x, full, full, full, full, rate, bias)

    vmem = pl.BlockSpec(memory_space=pltpu.VMEM)
    return pl.pallas_call(
        functools.partial(return_kernel, streams, places, heads),
        out_shape=jax.ShapeDtypeStruct((local, HEADS * DV), BF16),
        in_specs=[vmem] * 4,
        out_specs=any_space,
        scratch_shapes=[
            pltpu.VMEM((heads, DK + DV, DK), F32),
            pltpu.VMEM((heads, DK + DV, DK), F32),
            pltpu.VMEM((chips, heads, DK + DV, DK), F32),
            pltpu.VMEM((heads, DV, DK), F32),
            pltpu.VMEM((heads, DV, DK), F32),
            pltpu.VMEM((streams, local, heads * DV), BF16),
            dma((2,)),
            dma((2,)),
            dma((chips,)),
            dma((chips,)),
            dma((streams,)),
            dma((streams,)),
            dma((1,)),
        ],
        compiler_params=pltpu.CompilerParams(collective_id=1, has_side_effects=True),
    )(read, moved, maps, norm_gain[None])


def solution(mesh):
    return jax.shard_map(
        shards,
        mesh=mesh,
        in_specs=(
            P(("tm", "stream"), None),
            P("stream", None),
            P("stream", None),
            P("stream", None),
            P("stream", None),
            P("stream", None),
            P(),
            P(),
            P(),
        ),
        out_specs=P(("tm", "stream"), None),
        check_vma=False,
    )
```

```python
import functools

import jax
import jax.numpy as jnp
from jax import lax
from jax.experimental import pallas as pl
from jax.experimental.pallas import tpu as pltpu
from jax.sharding import PartitionSpec as P

HEADS = 16
DK = 128
DV = 128
CHUNK = 128
LANES = 128
F32 = jnp.float32
BF16 = jnp.bfloat16


def halves(a):
    high = a.astype(BF16)
    return high, (a - high.astype(F32)).astype(BF16)


def contract(a, b, dims):
    return lax.dot_general(a, b, dims, preferred_element_type=F32)


def dot3(a, b, ca, cb, batch=0):
    ah, al = halves(a)
    bh, bl = halves(b)
    free = batch + (cb - batch + 1) % 2
    lead = tuple(range(batch))
    wide = jnp.concatenate([bh, bl], free)
    both = contract(
        jnp.concatenate([ah, al], ca),
        jnp.concatenate([wide, wide], cb),
        (((ca,), (cb,)), (lead, lead)),
    )
    half = both.shape[-1] // 2
    return both[..., :half] + both[..., half:]


def around(count):
    return sorted(range(1, count), key=lambda i: min(i, count - i))


def gather_kernel(
    streams,
    places,
    heads,
    tok_ref,
    wq_ref,
    wk_ref,
    wv_ref,
    wg_ref,
    x_ref,
    full_ref,
    stage,
    load_sem,
    own_sem,
    tok_recv,
    right_sem,
    left_sem,
    cross_send,
    cross_recv,
    plane_send,
    pass_send,
    plane_recv,
):
    t = lax.axis_index("tm")
    z = lax.axis_index("stream")
    chips = places // 2
    chip = t // 2
    core = t % 2
    group = heads * DK

    loads = []
    for dest in range(streams):
        for j, ref in enumerate((wq_ref, wk_ref, wv_ref)):
            loads.append(
                pltpu.make_async_copy(
                    ref.at[t, :, pl.ds(dest * group, group)],
                    stage.at[dest, :, pl.ds(j * group, group)],
                    load_sem.at[dest, j],
                )
            )
        loads.append(
            pltpu.make_async_copy(
                wg_ref.at[t], stage.at[dest, :, pl.ds(3 * group, LANES)], load_sem.at[dest, 3]
            )
        )
    for copy in loads:
        copy.start()

    others = [(lax.rem(chip + i, chips) * 2 + core) for i in range(1, chips)]
    sibling = chip * 2 + 1 - core
    peers = [(t, lax.rem(z + i, streams)) for i in around(streams)]
    peers += [(sibling, z)] + [(o, z) for o in others]
    barrier = pltpu.get_barrier_semaphore()
    for peer in peers:
        pl.semaphore_signal(
            barrier, inc=1, device_id=peer, device_id_type=pl.DeviceIdType.MESH
        )
    pl.semaphore_wait(barrier, len(peers))
    for copy in loads:
        copy.wait()

    def remote(src, dst, send, recv, device):
        return pltpu.make_async_remote_copy(
            src_ref=src,
            dst_ref=dst,
            send_sem=send,
            recv_sem=recv,
            device_id=device,
            device_id_type=pl.DeviceIdType.MESH,
        )

    def cross(i):
        dest = lax.rem(z + i, streams)
        return remote(
            stage.at[dest], full_ref.at[t, z], cross_send.at[dest], cross_recv.at[z], (t, dest)
        )

    def crossed(i):
        s = lax.rem(z + i, streams)
        return remote(
            stage.at[s], full_ref.at[t, s], cross_send.at[s], cross_recv.at[s], (t, s)
        )

    def line(chunk, right, first):
        src = tok_ref if first else x_ref.at[chunk]
        send = (right_sem if right else left_sem).at[chunk]
        return remote(
            src, x_ref.at[chunk], send, tok_recv.at[chunk], (t, z + 1 if right else z - 1)
        )

    def plane(i, s, first):
        to = sibling if i == 0 else others[i - 1]
        src = stage.at[z] if first else full_ref.at[t, s]
        return remote(
            src, full_ref.at[t, s], plane_send.at[i, s], plane_recv.at[t, s], (to, z)
        )

    def relay(i, s):
        at = others[i - 1]
        here = full_ref.at[at, s]
        return remote(here, here, pass_send.at[i, s], plane_recv.at[at, s], (sibling, z))

    def landed(at, s):
        here = full_ref.at[at, s]
        return remote(here, here, plane_send.at[0, s], plane_recv.at[at, s], (sibling, z))

    for i in around(streams):
        cross(i).start()

    @pl.when(z < streams - 1)
    def _():
        line(z, True, True).start()

    @pl.when(z > 0)
    def _():
        line(z, False, True).start()

    for i in range(1, chips):
        plane(i, z, True).start()
    plane(0, z, True).start()
    own = [
        pltpu.make_async_copy(stage.at[z], full_ref.at[t, z], own_sem.at[0]),
        pltpu.make_async_copy(tok_ref, x_ref.at[z], own_sem.at[1]),
    ]
    for copy in own:
        copy.start()

    for i in around(streams):
        s = lax.rem(z + i, streams)
        crossed(i).wait_recv()
        for j in range(1, chips):
            plane(j, s, False).start()
        plane(0, s, False).start()

    def step(k):
        @pl.when(z >= k)
        def _():
            line(z - k, True, False).wait_recv()

            @pl.when(z < streams - 1)
            def _():
                line(z - k, True, False).start()

        @pl.when(z + k < streams)
        def _():
            line(z + k, False, False).wait_recv()

            @pl.when(z > 0)
            def _():
                line(z + k, False, False).start()

    orders = [z] + [lax.rem(z + i, streams) for i in around(streams)]
    passed = 0
    for k in range(1, streams):
        step(k)
        upto = len(orders) if k == streams - 2 else passed + 1
        while passed < min(upto, len(orders)):
            s = orders[passed]
            for i in range(1, chips):
                landed(others[i - 1], s).wait_recv()
                relay(i, s).start()
            passed += 1
    while passed < len(orders):
        s = orders[passed]
        for i in range(1, chips):
            landed(others[i - 1], s).wait_recv()
            relay(i, s).start()
        passed += 1

    for copy in own:
        copy.wait()
    for s in orders:
        landed(sibling, s).wait_recv()
        for i in range(1, chips):
            landed(lax.rem(chip + i, chips) * 2 + 1 - core, s).wait_recv()
    for i in around(streams):
        cross(i).wait_send()
    for n, s in enumerate(orders):
        for i in range(chips):
            plane(i, s, n == 0).wait_send()
        for i in range(1, chips):
            relay(i, s).wait_send()
    for k in range(streams):

        @pl.when((z >= k) & (z < streams - 1))
        def _():
            line(z - k, True, k == 0).wait_send()

        @pl.when((z + k < streams) & (z > 0))
        def _():
            line(z + k, False, k == 0).wait_send()


def block_kernel(
    heads,
    x_ref,
    w_ref,
    rate_ref,
    bias_ref,
    read_ref,
    query_ref,
    state_ref,
    cum,
    cum_row,
    beta,
):
    first_head = lax.axis_index("stream") * heads
    rows = x_ref.shape[0]
    places, streams, share, _ = w_ref.shape
    depth = places * share

    def project(groups):
        total = None
        for s in range(streams):
            parts = [w_ref[:, s, :, pl.ds(pl.multiple_of(at * LANES, LANES), LANES)] for at in groups]
            w = jnp.concatenate([part.reshape(depth, LANES) for part in parts], 1)
            term = contract(x_ref[:, s * depth : (s + 1) * depth], w, (((1,), (0,)), ((), ())))
            total = term if total is None else total + term
        return total

    chunks = rows // CHUNK
    row_at = lax.broadcasted_iota(jnp.int32, (CHUNK, CHUNK), 0)
    col_at = lax.broadcasted_iota(jnp.int32, (CHUNK, CHUNK), 1)

    logits = project((3 * heads,))
    soft = jnp.maximum(logits, 0.0) + jnp.log1p(jnp.exp(-jnp.abs(logits)))
    decay = (-rate_ref[...] * soft).astype(BF16)
    beta[...] = (
        (1.0 / (1.0 + jnp.exp(-(logits + bias_ref[...])))).astype(BF16).astype(F32)
    ).reshape(chunks, CHUNK, LANES)
    lower_ones = jnp.where(row_at >= col_at, 1.0, 0.0).astype(BF16)
    for c in range(chunks):
        piece = decay[c * CHUNK : (c + 1) * CHUNK]
        sums = contract(lower_ones, piece, (((1,), (0,)), ((), ())))
        cum[c] = sums
        cum_row[c] = sums.T

    qs, ks, vs, gs, bs, g_rows = [], [], [], [], [], []
    lane = lax.broadcasted_iota(jnp.int32, (chunks, CHUNK, LANES), 2)
    for h in range(heads):
        raw = project([h + j * heads for j in range(3)])
        raw_q = raw[:, :DK]
        raw_k = raw[:, DK : 2 * DK]
        q = (
            raw_q * lax.rsqrt(jnp.sum(raw_q * raw_q, -1, keepdims=True) + 1e-06) * DK ** (-0.5)
        ).astype(BF16)
        k = (raw_k * lax.rsqrt(jnp.sum(raw_k * raw_k, -1, keepdims=True) + 1e-06)).astype(BF16)
        v = raw[:, 2 * DK :].astype(BF16)
        qs.append(q.reshape(chunks, CHUNK, DK))
        ks.append(k.reshape(chunks, CHUNK, DK))
        vs.append(v.reshape(chunks, CHUNK, DV))
        head = first_head + h
        gs.append(jnp.sum(jnp.where(lane == head, cum[...], 0.0), -1, keepdims=True))
        bs.append(jnp.sum(jnp.where(lane == head + HEADS, beta[...], 0.0), -1, keepdims=True))
        g_rows.append(cum_row[:, pl.ds(head, 1), :])
    q, k, v, g, b, g_row = (jnp.concatenate(a, 0) for a in (qs, ks, vs, gs, bs, g_rows))
    v = v.astype(F32)
    g_last = g[:, CHUNK - 1 :, :]
    growth = jnp.exp(g)
    tail = jnp.exp(g_last - g)
    whole = jnp.exp(g_last)

    batched = (((2,), (2,)), ((0,), (0,)))
    pair = contract(jnp.concatenate([k, q], 1), k, batched)
    low = row_at >= col_at
    spread = jnp.exp(jnp.where(low[None], g - g_row, 0.0))
    lmat = jnp.where((row_at > col_at)[None], b * spread * pair[:, :CHUNK], 0.0)
    mmat = jnp.where(low[None], spread * pair[:, CHUNK:], 0.0)

    eye = jnp.where(row_at == col_at, 1.0, 0.0)
    inverse = None
    size = 1
    while size < CHUNK:
        inside = (row_at // (2 * size) == col_at // (2 * size)) & (row_at // size != col_at // size)
        off = jnp.where(inside[None], lmat, 0.0)
        if inverse is None:
            inverse = eye[None] - off
        else:
            inverse = inverse - dot3(inverse, dot3(off, inverse, 2, 1, 1), 2, 1, 1)
        size *= 2

    kf = k.astype(F32)
    right = jnp.concatenate([(b * growth) * kf, b * v], 2)
    wu = dot3(inverse, right, 2, 1, 1)
    mwu = dot3(mmat, wu, 2, 1, 1)
    moved = growth * q.astype(F32) - mwu[:, :, :DK]
    key_tail = tail * kf
    jumps = dot3(jnp.swapaxes(wu, 1, 2), key_tail, 2, 1, 1)
    step_map = whole * eye[None] - jumps[:, :DK]

    carries = [None] * heads
    for c in range(chunks):
        at = slice(c * CHUNK, (c + 1) * CHUNK)
        for h in range(heads):
            n = h * chunks + c
            lanes = slice(h * DK, (h + 1) * DK)
            if c == 0:
                query_ref[at, lanes] = moved[n]
                read_ref[at, lanes] = mwu[n, :, DK:]
                carries[h] = jnp.concatenate([step_map[n], jumps[n, DK:]], 0)
                continue
            both = dot3(moved[n], carries[h], 1, 1)
            query_ref[at, lanes] = both[:, :DK]
            read_ref[at, lanes] = mwu[n, :, DK:] + both[:, DK:]
            carry = dot3(carries[h], step_map[n], 1, 0)
            carries[h] = jnp.concatenate([carry[:DK], carry[DK:] + jumps[n, DK:]], 0)
    for h in range(heads):
        state_ref[h] = carries[h]


def return_kernel(
    streams,
    places,
    heads,
    read_ref,
    query_ref,
    maps_ref,
    gain_ref,
    out_ref,
    pair,
    total,
    got,
    carried,
    state,
    mixed,
    pair_sem,
    state_sem,
    chip_send,
    chip_recv,
    out_send,
    out_recv,
    own_sem,
):
    t = lax.axis_index("tm")
    z = lax.axis_index("stream")
    chips = places // 2
    chip = t // 2
    core = t % 2
    sibling = chip * 2 + 1 - core
    group = heads * DV
    local = out_ref.shape[0]

    peers = [(t, lax.rem(z + i, streams)) for i in around(streams)]
    peers += [(sibling, z)]
    peers += [(lax.rem(chip + i, chips) * 2 + core, z) for i in range(1, chips)]
    barrier = pltpu.get_barrier_semaphore()
    for peer in peers:
        pl.semaphore_signal(
            barrier, inc=1, device_id=peer, device_id_type=pl.DeviceIdType.MESH
        )
    pl.semaphore_wait(barrier, len(peers))

    def remote(src, dst, send, recv, device):
        return pltpu.make_async_remote_copy(
            src_ref=src,
            dst_ref=dst,
            send_sem=send,
            recv_sem=recv,
            device_id=device,
            device_id_type=pl.DeviceIdType.MESH,
        )

    def hand_over():
        return remote(maps_ref, pair, pair_sem.at[0], pair_sem.at[1], (sibling, z))

    def hand_back():
        return remote(carried, carried, state_sem.at[0], state_sem.at[1], (sibling, z))

    def to_chip(source, dest):
        src, dst = total, got.at[source]
        if source == 0:
            src, dst = total.at[:, pl.ds(DK, DV)], got.at[0, :, pl.ds(DK, DV)]
        return remote(src, dst, chip_send.at[dest], chip_recv.at[source], (dest * 2 + 1, z))

    @pl.when(core == 0)
    def _():
        hand_over().start()
        hand_over().wait_send()

    @pl.when(core == 1)
    def _():
        hand_over().wait_recv()

        @pl.when(chip < chips - 1)
        def _():
            for h in range(heads):
                both = dot3(pair[h], maps_ref[h, :DK], 1, 0)
                total[h, :DK] = both[:DK]
                total[h, DK:] = both[DK:] + maps_ref[h, DK:]

        for source in range(chips - 1):

            @pl.when(chip == source)
            def _():
                for dest in range(chips - 1, source, -1):
                    to_chip(source, dest).start()

        for source in range(chips - 1):

            @pl.when(chip > source)
            def _():
                to_chip(source, chip).wait_recv()
                for h in range(heads):
                    if source == 0:
                        carried[h] = got[0, h, DK:]
                    else:
                        carried[h] = dot3(carried[h], got[source, h, :DK], 1, 0) + got[source, h, DK:]

        @pl.when(chip > 0)
        def _():
            hand_back().start()
            for h in range(heads):
                state[h] = dot3(carried[h], pair[h, :DK], 1, 0) + pair[h, DK:]

        @pl.when(chip == 0)
        def _():
            for h in range(heads):
                state[h] = pair[h, DK:]

    @pl.when((core == 0) & (chip > 0))
    def _():
        hand_back().wait_recv()
        for h in range(heads):
            state[h] = carried[h]

    @pl.when((core == 0) & (chip == 0))
    def _():
        state[...] = jnp.zeros_like(state)

    def outgoing(i):
        dest = lax.rem(z + i, streams)
        dst = out_ref.at[:, pl.ds(pl.multiple_of(z * group, group), group)]
        return remote(mixed.at[dest], dst, out_send.at[dest], out_recv.at[z], (t, dest))

    def incoming(i):
        source = lax.rem(z + i, streams)
        dst = out_ref.at[:, pl.ds(pl.multiple_of(source * group, group), group)]
        return remote(mixed.at[source], dst, out_send.at[source], out_recv.at[source], (t, source))

    own = pltpu.make_async_copy(
        mixed.at[z], out_ref.at[:, pl.ds(pl.multiple_of(z * group, group), group)], own_sem.at[0]
    )
    order = list(reversed(around(streams)))
    for i in order + [0]:
        dest = lax.rem(z + i, streams)
        at = pl.ds(pl.multiple_of(dest * local, local), local)
        for h in range(heads):
            lanes = slice(h * DV, (h + 1) * DV)
            read = read_ref[at, lanes] + dot3(query_ref[at, lanes], state[h], 1, 1)
            readout = read.astype(BF16).astype(F32)
            scale = lax.rsqrt(jnp.mean(readout * readout, -1, keepdims=True) + 1e-06)
            mixed[dest, :, lanes] = (readout * scale * gain_ref[...]).astype(BF16)
        if i == 0:
            own.start()
        else:
            outgoing(i).start()

    own.wait()
    for i in order:
        incoming(i).wait_recv()
    for i in order:
        outgoing(i).wait_send()

    @pl.when((core == 1) & (chip > 0))
    def _():
        hand_back().wait_send()

    for source in range(chips - 1):

        @pl.when((core == 1) & (chip == source))
        def _():
            for dest in range(chips - 1, source, -1):
                to_chip(source, dest).wait_send()


def shards(
    tokens, w_query, w_key, w_value, decay_proj, beta_proj, decay_rate, beta_bias, norm_gain
):
    streams = lax.axis_size("stream")
    places = lax.axis_size("tm")
    heads = HEADS // streams
    depth = w_query.shape[0]
    share = depth // places
    width = 3 * heads * DK + LANES
    gates = jnp.pad(
        jnp.concatenate([decay_proj, beta_proj], 1), ((0, 0), (0, LANES - 2 * HEADS))
    )
    shares = [w.reshape(places, share, -1) for w in (w_query, w_key, w_value, gates)]
    local, features = tokens.shape
    any_space = pl.BlockSpec(memory_space=pl.ANY)
    dma = pltpu.SemaphoreType.DMA
    chips = places // 2
    x, full = pl.pallas_call(
        functools.partial(gather_kernel, streams, places, heads),
        out_shape=(
            jax.ShapeDtypeStruct((streams, local, features), BF16),
            jax.ShapeDtypeStruct((places, streams, share, width), BF16),
        ),
        in_specs=[pl.BlockSpec(memory_space=pltpu.VMEM)] + [any_space] * 4,
        out_specs=(any_space, any_space),
        scratch_shapes=[
            pltpu.VMEM((streams, share, width), BF16),
            dma((streams, 4)),
            dma((2,)),
            dma((streams,)),
            dma((streams,)),
            dma((streams,)),
            dma((streams,)),
            dma((streams,)),
            dma((chips, streams)),
            dma((chips, streams)),
            dma((places, streams)),
        ],
        compiler_params=pltpu.CompilerParams(collective_id=0, has_side_effects=True),
    )(tokens, *shares)
    x = x.reshape(streams * local, features)
    rows = x.shape[0]
    if share % 16:
        full = full.transpose(1, 0, 2, 3).reshape(1, streams, places * share, width)

    rate = jnp.pad(decay_rate, (0, LANES - HEADS))[None]
    bias = jnp.pad(beta_bias, (HEADS, LANES - 2 * HEADS))[None]

    chunks = rows // CHUNK
    read, moved, maps = pl.pallas_call(
        functools.partial(block_kernel, heads),
        out_shape=(
            jax.ShapeDtypeStruct((rows, heads * DV), F32),
            jax.ShapeDtypeStruct((rows, heads * DK), F32),
            jax.ShapeDtypeStruct((heads, DK + DV, DK), F32),
        ),
        in_specs=[pl.BlockSpec(memory_space=pltpu.VMEM)] * 4,
        out_specs=(pl.BlockSpec(memory_space=pltpu.VMEM),) * 3,
        scratch_shapes=[
            pltpu.VMEM((chunks, CHUNK, LANES), F32),
            pltpu.VMEM((chunks, LANES, CHUNK), F32),
            pltpu.VMEM((chunks, CHUNK, LANES), F32),
        ],
    )(x, full, rate, bias)

    vmem = pl.BlockSpec(memory_space=pltpu.VMEM)
    return pl.pallas_call(
        functools.partial(return_kernel, streams, places, heads),
        out_shape=jax.ShapeDtypeStruct((local, HEADS * DV), BF16),
        in_specs=[vmem] * 4,
        out_specs=any_space,
        scratch_shapes=[
            pltpu.VMEM((heads, DK + DV, DK), F32),
            pltpu.VMEM((heads, DK + DV, DK), F32),
            pltpu.VMEM((chips, heads, DK + DV, DK), F32),
            pltpu.VMEM((heads, DV, DK), F32),
            pltpu.VMEM((heads, DV, DK), F32),
            pltpu.VMEM((streams, local, heads * DV), BF16),
            dma((2,)),
            dma((2,)),
            dma((chips,)),
            dma((chips,)),
            dma((streams,)),
            dma((streams,)),
            dma((1,)),
        ],
        compiler_params=pltpu.CompilerParams(collective_id=1, has_side_effects=True),
    )(read, moved, maps, norm_gain[None])


def solution(mesh):
    return jax.shard_map(
        shards,
        mesh=mesh,
        in_specs=(
            P(("tm", "stream"), None),
            P("stream", None),
            P("stream", None),
            P("stream", None),
            P("stream", None),
            P("stream", None),
            P(),
            P(),
            P(),
        ),
        out_specs=P(("tm", "stream"), None),
        check_vma=False,
    )
```
